32 devices in a mesh: row: 4 (over y, core), col: 8 (over z, x).
Axes of the slice: x: 2, y: 2, z: 4, core: 2. Of those that a mesh axis runs over, the one named last changes fastest.
Arguments:
- gram_matrix: float32 [12288, 12288], P('row', 'col'), may hold values from -1 to 16, as said below
- targets: float32 [10, 12288], P(None, ('row', 'col')), may hold values from -10 to 10
Outputs:
- solution: float32 [10, 12288], P(None, ('row', 'col'))
- residual: float32 [10, 12288], P(None, ('row', 'col'))
The draws below stay inside these ranges and needn't reach their ends.
Inputs may be any that keep to these rules, and one draw needn't show every extreme that they name: With its columns put back in sample order as in the first step, gram_matrix is symmetric positive definite.
All inputs are finite; a program needn't handle non-finite values.
Results may differ from the reference program's by a relative error of at most 0.0003.
Values sent between devices are 32-bit elements; how exact they have to be, the bound alone decides.
A program may use at most 64 MiB of HBM per device.

```python
import math
import jax
import jax.numpy as jnp
from jax import lax

N = 12288
CLASSES = 10
ITERS = 2
PIECE = 384
N_ROW = 4
N_COL = 8


def draw_gram_matrix(key, part):
    noise_key, ridge_key = jax.random.split(jax.random.fold_in(key, 17), 2)
    noise = jnp.clip(jax.random.normal(noise_key, (N, N), jnp.float32), -6.0, 6.0)
    whole = (noise + noise.T) * (0.45 / math.sqrt(2.0 * N))
    ridge = jnp.exp(jax.random.uniform(ridge_key, (N,), jnp.float32, math.log(1.2), math.log(4.0)))
    places = jnp.arange(N, dtype=jnp.int32)
    whole = whole.at[places, places].add(ridge)
    blocks = whole.reshape(N, N_ROW, N_COL, PIECE)
    return jnp.transpose(blocks, (0, 2, 1, 3)).reshape(N, N)


def draw_targets(key, part):
    base_key = jax.random.fold_in(jax.random.fold_in(key, 29), 0)
    position = jnp.arange(N, dtype=jnp.float32) / N
    ramp = 0.6 + 1.2 * position
    values = jnp.clip(jax.random.normal(base_key, (CLASSES, N), jnp.float32), -5.0, 5.0)
    return values * ramp


def setup_inputs(seed: int = 0) -> dict:
    key_of = jax.random.split(jax.random.key(seed), 3)
    return {
        "gram_matrix": draw_gram_matrix(jax.random.fold_in(key_of[2], 71), 0),
        "targets": draw_targets(jax.random.fold_in(key_of[2], 71), 0),
    }


def apply_gram(gram_matrix, vectors):
    mixed = jnp.dot(vectors, gram_matrix, precision=lax.Precision.HIGHEST, preferred_element_type=jnp.float32)
    classes = vectors.shape[0]
    blocks = mixed.reshape(classes, N_COL, N_ROW, PIECE)
    return jnp.transpose(blocks, (0, 2, 1, 3)).reshape(classes, N)


def reference(gram_matrix, targets):
    solution = jnp.zeros_like(targets)
    residual = targets
    direction = targets
    norm_now = jnp.sum(residual * residual, axis=1)
    for iteration in range(ITERS):
        mapped = apply_gram(gram_matrix, direction)
        step_size = norm_now / jnp.sum(direction * mapped, axis=1)
        solution = solution + step_size[:, None] * direction
        residual = residual - step_size[:, None] * mapped
        norm_next = jnp.sum(residual * residual, axis=1)
        direction = residual + (norm_next / norm_now)[:, None] * direction
        norm_now = norm_next
    return solution, residual
```

```python
import functools

import jax
import jax.numpy as jnp
from jax import lax
from jax.experimental import pallas as pl
from jax.experimental.pallas import tpu as pltpu
from jax.sharding import PartitionSpec as P

ITERS = 2
LANES = 128
SUB = 8
DEPTH = 256
MESH = pl.DeviceIdType.MESH
F32 = jnp.float32
BF16 = jnp.bfloat16


def dot(a, b):
    return lax.dot_general(a, b, (((1,), (0,)), ((), ())), preferred_element_type=F32)


def halves(x):
    high = x.astype(BF16)
    return high, (x - high.astype(F32)).astype(BF16)


def kernel(
    n_row, n_col, classes, piece, group,
    gram, targets, sol_out, res_out,
    stage, high, low, acc, vec, wide,
    t_col, t_row, w_part, w_col, w_row, m_part, moments, finals,
    gram_sem, s_tcol, r_tcol, s_trow, r_trow, s_rs, r_rs, s_wcol, r_wcol, s_wrow, r_wrow,
    s_rs2, r_rs2, s_mom, r_mom, s_fin, r_fin,
):
    row, col = lax.axis_index("row"), lax.axis_index("col")
    rest = classes - SUB
    tiles = piece // LANES
    n_dev = n_row * n_col
    n_group = n_col // group
    own_group = col // group
    depth = group * piece
    order = [0]
    for k in range(1, n_group):
        order.append((k + 1) // 2 if k % 2 else n_group - k // 2)
    groups = [lax.rem(own_group + k, n_group) for k in order]

    for i in range(n_group):
        pltpu.make_async_copy(
            gram.at[pl.ds(pl.multiple_of(groups[i] * depth, DEPTH), depth)], stage.at[i], gram_sem.at[i]
        ).start()

    barrier = pltpu.get_barrier_semaphore()

    def greet(k, carry):
        other = lax.rem(row * n_col + col + k, n_dev)
        pl.semaphore_signal(barrier, inc=1, device_id=(other // n_col, lax.rem(other, n_col)), device_id_type=MESH)
        return carry

    lax.fori_loop(1, n_dev, greet, 0)

    rows8 = lax.broadcasted_iota(jnp.int32, (SUB, LANES), 0)

    def pack(x):
        extra = jnp.zeros((SUB, LANES), F32)
        for i in range(tiles):
            part = x[SUB:, i * LANES:(i + 1) * LANES]
            if i:
                part = pltpu.roll(part, rest * i, 0)
            extra = jnp.where((rows8 >= rest * i) & (rows8 < rest * (i + 1)), part, extra)
        return jnp.concatenate([x[:SUB], extra], axis=1)

    def unpack(y):
        extra = y[:, piece:]
        parts = []
        for i in range(tiles):
            part = pltpu.roll(extra, SUB - rest * i, 0) if i else extra
            parts.append(jnp.where(rows8 < rest, part, 0.0))
        return jnp.concatenate([y[:, :piece], jnp.concatenate(parts, axis=1)], axis=0)

    def to_col(src, dst, send, recv, k):
        return pltpu.make_async_remote_copy(
            src_ref=src, dst_ref=dst, send_sem=send.at[k], recv_sem=recv.at[k],
            device_id=(row, lax.rem(col + k, n_col)), device_id_type=MESH)

    def to_row(src, dst, send, recv, k):
        return pltpu.make_async_remote_copy(
            src_ref=src, dst_ref=dst, send_sem=send.at[k], recv_sem=recv.at[k],
            device_id=(lax.rem(row + k, n_row), col), device_id_type=MESH)

    started = []

    def go(copy):
        copy.start()
        started.append(copy)
        return copy

    wide[...] = jnp.zeros_like(wide)
    wide[0:classes, :] = targets[...]
    mine_t = wide[...]
    t_col[0] = pack(mine_t)
    acc[...] = jnp.zeros_like(acc)
    pl.semaphore_wait(barrier, n_dev - 1)

    col_t = {k: go(to_col(t_col.at[0], t_col.at[k], s_tcol, r_tcol, k)) for k in range(1, n_col)}
    row_t = {k: go(to_row(t_col.at[0], t_row.at[k], s_trow, r_trow, k)) for k in range(1, n_row)}

    def gather(i, pieces, send, recv):
        for j in range(group):
            source = groups[i] * group + j
            slot = lax.rem(col - source + n_col, n_col)

            @pl.when(slot != 0)
            def _():
                to_col(pieces.at[0], pieces.at[slot], send, recv, slot).wait_recv()

            x = unpack(pieces[slot])
            a, b = halves(x)
            vec[i, :, j * piece:(j + 1) * piece] = jnp.concatenate([a, b], axis=0)

    def accumulate(v, h, l):
        both = dot(v, h)
        acc[...] += both[:16] + both[16:] + dot(v[:16], l)

    for i in range(n_group):
        pltpu.make_async_copy(gram.at[pl.ds(0, depth)], stage.at[i], gram_sem.at[i]).wait()
        gather(i, t_col, s_tcol, r_tcol)

        def first(j, carry, i=i):
            off = pl.ds(pl.multiple_of(j * DEPTH, DEPTH), DEPTH)
            h, l = halves(stage[i, off, :])
            high[i, off, :] = h
            low[i, off, :] = l
            accumulate(vec[i, :, off], h, l)
            return carry

        lax.fori_loop(0, depth // DEPTH, first, 0)

    def columns(k):
        r = lax.rem(row - k + n_row, n_row)
        return pl.ds(pl.multiple_of(r * piece, LANES), piece)

    def scatter(parts, send, recv):
        copies = {}
        for k in range(1, n_row):
            r = lax.rem(row + k, n_row)
            parts[n_row + k] = pack(acc[:, pl.ds(pl.multiple_of(r * piece, LANES), piece)])
            copies[k] = go(to_row(parts.at[n_row + k], parts.at[k], send, recv, k))
        return copies

    rs = scatter(w_part, s_rs, r_rs)
    total = pack(acc[:, columns(0)])
    for k in range(1, n_row):
        rs[k].wait_recv()
        total = total + w_part[k]
    w_col[0] = total
    col_w = {k: go(to_col(w_col.at[0], w_col.at[k], s_wcol, r_wcol, k)) for k in range(1, n_col)}
    row_w = {k: go(to_row(w_col.at[0], w_row.at[k], s_wrow, r_wrow, k)) for k in range(1, n_row)}
    acc[...] = jnp.zeros_like(acc)
    mine_w = unpack(total)

    ts, ws = [mine_t], [mine_w]
    for k in range(1, n_row):
        row_t[k].wait_recv()
        row_w[k].wait_recv()
        ts.append(unpack(t_row[k]))
        ws.append(unpack(w_row[k]))

    def inner(xs, ys):
        value = xs[0] * ys[0]
        for x, y in zip(xs[1:], ys[1:]):
            value = value + x * y
        return jnp.sum(value, axis=1, keepdims=True)

    lane = lax.broadcasted_iota(jnp.int32, (16, LANES), 1)
    sub = lax.broadcasted_iota(jnp.int32, (16, LANES), 0)

    def to_lanes(values):
        out = jnp.zeros((16, LANES), F32)
        for m, value in enumerate(values):
            out = jnp.where(lane == sub + 16 * m, value, out)
        return jnp.sum(out, axis=0, keepdims=True)

    def from_lanes(line, m):
        full = jnp.broadcast_to(line, (16, LANES))
        return jnp.sum(jnp.where(lane == sub + 16 * m, full, 0.0), axis=1, keepdims=True)

    tt, tw, ww = inner(ts, ts), inner(ts, ws), inner(ws, ws)
    guess = jnp.where(ww > 0.0, tw / jnp.where(ww > 0.0, ww, 1.0), 0.0)
    rs0 = [t - guess * w for t, w in zip(ts, ws)]
    rr, rw = inner(rs0, rs0), inner(rs0, ws)
    moments[0] = to_lanes([tt, tw, ww, guess, rr, rw])
    col_m = {k: go(to_col(moments.at[0], moments.at[k], s_mom, r_mom, k)) for k in range(1, n_col)}

    for i in range(n_group):
        gather(i, w_col, s_wcol, r_wcol)

        def second(j, carry, i=i):
            off = pl.ds(pl.multiple_of(j * DEPTH, DEPTH), DEPTH)
            accumulate(vec[i, :, off], high[i, off, :], low[i, off, :])
            return carry

        lax.fori_loop(0, depth // DEPTH, second, 0)

    rs2 = scatter(m_part, s_rs2, r_rs2)

    for k in range(1, n_col):
        col_m[k].wait_recv()
    known = [[from_lanes(moments[k], m) for m in range(6)] for k in range(n_col)]

    def add(values):
        out = values[0]
        for v in values[1:]:
            out = out + v
        return out

    norm0 = add([m[0] for m in known])
    t_k_t = add([m[1] for m in known])
    step0 = norm0 / t_k_t
    shift = [step0 - m[3] for m in known]
    norm1 = add([m[4] - d * (2.0 * m[5] - d * m[2]) for m, d in zip(known, shift)])
    r_w = add([m[5] - d * m[2] for m, d in zip(known, shift)])
    beta = norm1 / norm0

    def direction(t, w):
        r = t - step0 * w
        return r, r + beta * t

    ds = [direction(t, w)[1] for t, w in zip(ts, ws)]
    ps = [acc[:, columns(k)] for k in range(n_row)]
    finals[0] = to_lanes([inner(ds, ps)])

    def fin(k):
        other = lax.rem(row * n_col + col + k, n_dev)
        return pltpu.make_async_remote_copy(
            src_ref=finals.at[0], dst_ref=finals.at[k], send_sem=s_fin.at[k], recv_sem=r_fin.at[k],
            device_id=(other // n_col, lax.rem(other, n_col)), device_id_type=MESH)

    def fin_start(k, carry):
        fin(k).start()
        return carry

    lax.fori_loop(1, n_dev, fin_start, 0)

    total2 = pack(acc[:, columns(0)])
    for k in range(1, n_row):
        rs2[k].wait_recv()
        total2 = total2 + m_part[k]
    w2 = unpack(total2)
    r1, d1 = direction(mine_t, mine_w)
    mapped = (1.0 + beta) * mine_w - step0 * w2

    def fin_wait(k, carry):
        fin(k).wait_recv()
        return carry

    lax.fori_loop(1, n_dev, fin_wait, 0)
    d_w2 = from_lanes(jnp.sum(finals[...], axis=0), 0)
    step1 = norm1 / ((1.0 + beta) * (r_w + beta * t_k_t) - step0 * d_w2)
    wide[...] = step0 * mine_t + step1 * d1
    sol_out[...] = wide[0:classes, :]
    wide[...] = r1 - step1 * mapped
    res_out[...] = wide[0:classes, :]

    for copy in started:
        copy.wait_send()

    def fin_sent(k, carry):
        fin(k).wait_send()
        return carry

    lax.fori_loop(1, n_dev, fin_sent, 0)


def fused(n_row, n_col, gram_matrix, targets):
    classes, piece = targets.shape
    height, width = gram_matrix.shape
    group = 1 if piece % DEPTH == 0 else 2
    n_group = n_col // group
    depth = group * piece
    packed = (SUB, piece + LANES)
    dma = pltpu.SemaphoreType.DMA
    n_dev = n_row * n_col
    vmem = pl.BlockSpec(memory_space=pltpu.VMEM)
    return pl.pallas_call(
        functools.partial(kernel, n_row, n_col, classes, piece, group),
        out_shape=[jax.ShapeDtypeStruct(targets.shape, F32)] * 2,
        in_specs=[pl.BlockSpec(memory_space=pl.ANY), vmem],
        out_specs=[vmem, vmem],
        scratch_shapes=[
            pltpu.VMEM((n_group, depth, width), F32),
            pltpu.VMEM((n_group, depth, width), BF16),
            pltpu.VMEM((n_group, depth, width), BF16),
            pltpu.VMEM((16, width), F32),
            pltpu.VMEM((n_group, 32, depth), BF16),
            pltpu.VMEM((16, piece), F32),
            pltpu.VMEM((n_col,) + packed, F32),
            pltpu.VMEM((n_row,) + packed, F32),
            pltpu.VMEM((2 * n_row,) + packed, F32),
            pltpu.VMEM((n_col,) + packed, F32),
            pltpu.VMEM((n_row,) + packed, F32),
            pltpu.VMEM((2 * n_row,) + packed, F32),
            pltpu.VMEM((n_col, 1, LANES), F32),
            pltpu.VMEM((n_dev, 1, LANES), F32),
            dma((n_group,)),
            dma((n_col,)), dma((n_col,)), dma((n_row,)), dma((n_row,)),
            dma((n_row,)), dma((n_row,)),
            dma((n_col,)), dma((n_col,)), dma((n_row,)), dma((n_row,)),
            dma((n_row,)), dma((n_row,)),
            dma((n_col,)), dma((n_col,)),
            dma((n_dev,)), dma((n_dev,)),
        ],
        compiler_params=pltpu.CompilerParams(
            collective_id=0, has_side_effects=True, vmem_limit_bytes=60 * 2**20
        ),
    )(gram_matrix, targets)


def fits(n_row, n_col, gram_matrix, targets):
    classes, piece = targets.shape
    rest = classes - SUB
    group = 1 if piece % DEPTH == 0 else 2
    return (
        piece % LANES == 0
        and 0 < rest <= SUB
        and rest * (piece // LANES) <= SUB
        and n_col % group == 0
        and (group * piece) % DEPTH == 0
        and gram_matrix.size * 8 <= 48 * 2**20
    )


def apply_gram(gram_matrix, vectors):
    partial_value = jnp.dot(
        vectors, gram_matrix, precision=lax.Precision.HIGHEST, preferred_element_type=jnp.float32
    )
    mapped = lax.psum_scatter(partial_value, "row", scatter_dimension=1, tiled=True)
    mapped = lax.all_gather(mapped, "col", axis=1, tiled=True)
    return mapped


def class_sums(values):
    return lax.psum(values, "row")


def shards(gram_matrix, targets):
    piece_len = targets.shape[1]
    known = lax.all_gather(targets, "col", axis=1, tiled=True)
    solution = jnp.zeros_like(known)
    residual = known
    direction = known
    norm_now = class_sums(jnp.sum(residual * residual, axis=1))
    for iteration in range(ITERS):
        mapped = apply_gram(gram_matrix, direction)
        step_size = norm_now / class_sums(jnp.sum(direction * mapped, axis=1))
        solution = solution + step_size[:, None] * direction
        residual = residual - step_size[:, None] * mapped
        norm_next = class_sums(jnp.sum(residual * residual, axis=1))
        direction = residual + (norm_next / norm_now)[:, None] * direction
        norm_now = norm_next
    offset = lax.axis_index("col") * piece_len
    solution = lax.dynamic_slice_in_dim(solution, offset, piece_len, 1)
    residual = lax.dynamic_slice_in_dim(residual, offset, piece_len, 1)
    return (solution, residual)


def solution(mesh):
    n_row, n_col = mesh.shape["row"], mesh.shape["col"]

    def local(gram_matrix, targets):
        if fits(n_row, n_col, gram_matrix, targets):
            return tuple(fused(n_row, n_col, gram_matrix, targets))
        return shards(gram_matrix, targets)

    in_specs = (P("row", "col"), P(None, ("row", "col")))
    out_specs = (P(None, ("row", "col")), P(None, ("row", "col")))
    return jax.shard_map(local, mesh=mesh, in_specs=in_specs, out_specs=out_specs, check_vma=False)
```

```python
import functools

import jax
import jax.numpy as jnp
from jax import lax
from jax.experimental import pallas as pl
from jax.experimental.pallas import tpu as pltpu
from jax.sharding import PartitionSpec as P

ITERS = 2
LANES = 128
SUB = 8
DEPTH = 256
MESH = pl.DeviceIdType.MESH
F32 = jnp.float32
BF16 = jnp.bfloat16


def dot(a, b):
    return lax.dot_general(a, b, (((1,), (0,)), ((), ())), preferred_element_type=F32)


def halves(x):
    high = x.astype(BF16)
    return high, (x - high.astype(F32)).astype(BF16)


def kernel(
    n_row, n_col, classes, piece, group,
    gram, targets, both_out,
    stage, high, low, acc, vec, wide,
    t_col, t_row, w_part, w_col, w_row, m_part, moments, finals,
    gram_sem, s_tcol, r_tcol, s_trow, r_trow, s_rs, r_rs, s_wcol, r_wcol, s_wrow, r_wrow,
    s_rs2, r_rs2, s_mom, r_mom, s_fin, r_fin,
):
    row, col = lax.axis_index("row"), lax.axis_index("col")
    rest = classes - SUB
    tiles = piece // LANES
    n_dev = n_row * n_col
    n_group = n_col // group
    own_group = col // group
    depth = group * piece
    order = [0]
    for k in range(1, n_group):
        order.append((k + 1) // 2 if k % 2 else n_group - k // 2)
    groups = [lax.rem(own_group + k, n_group) for k in order]

    for i in range(n_group):
        pltpu.make_async_copy(
            gram.at[pl.ds(pl.multiple_of(groups[i] * depth, DEPTH), depth)], stage.at[i], gram_sem.at[i]
        ).start()

    barrier = pltpu.get_barrier_semaphore()

    for k in range(1, n_col):
        pl.semaphore_signal(barrier, inc=1, device_id=(row, lax.rem(col + k, n_col)), device_id_type=MESH)
    for k in range(1, n_row):
        pl.semaphore_signal(barrier, inc=1, device_id=(lax.rem(row + k, n_row), col), device_id_type=MESH)

    rows8 = lax.broadcasted_iota(jnp.int32, (SUB, LANES), 0)

    def pack(x):
        extra = jnp.zeros((SUB, LANES), F32)
        for i in range(tiles):
            part = x[SUB:, i * LANES:(i + 1) * LANES]
            if i:
                part = pltpu.roll(part, rest * i, 0)
            extra = jnp.where((rows8 >= rest * i) & (rows8 < rest * (i + 1)), part, extra)
        return jnp.concatenate([x[:SUB], extra], axis=1)

    def unpack(y):
        extra = y[:, piece:]
        parts = []
        for i in range(tiles):
            part = pltpu.roll(extra, SUB - rest * i, 0) if i else extra
            parts.append(jnp.where(rows8 < rest, part, 0.0))
        return jnp.concatenate([y[:, :piece], jnp.concatenate(parts, axis=1)], axis=0)

    def to_col(src, dst, send, recv, k):
        return pltpu.make_async_remote_copy(
            src_ref=src, dst_ref=dst, send_sem=send.at[k], recv_sem=recv.at[k],
            device_id=(row, lax.rem(col + k, n_col)), device_id_type=MESH)

    def to_row(src, dst, send, recv, k):
        return pltpu.make_async_remote_copy(
            src_ref=src, dst_ref=dst, send_sem=send.at[k], recv_sem=recv.at[k],
            device_id=(lax.rem(row + k, n_row), col), device_id_type=MESH)

    started = []

    def go(copy):
        copy.start()
        started.append(copy)
        return copy

    wide[...] = jnp.zeros_like(wide)
    wide[0:classes, :] = targets[...]
    mine_t = wide[...]
    t_col[0] = pack(mine_t)
    acc[...] = jnp.zeros_like(acc)
    pl.semaphore_wait(barrier, n_row + n_col - 2)

    col_t = {k: go(to_col(t_col.at[0], t_col.at[k], s_tcol, r_tcol, k)) for k in range(1, n_col)}
    row_t = {k: go(to_row(t_col.at[0], t_row.at[k], s_trow, r_trow, k)) for k in range(1, n_row)}

    def split(i):
        pltpu.make_async_copy(gram.at[pl.ds(0, depth)], stage.at[i], gram_sem.at[i]).wait()

        def part(j, carry):
            off = pl.ds(pl.multiple_of(j * DEPTH, DEPTH), DEPTH)
            high[i, off, :], low[i, off, :] = halves(stage[i, off, :])
            return carry

        lax.fori_loop(0, depth // DEPTH, part, 0)

    def gather(i, pieces, send, recv):
        for j in range(group):
            source = groups[i] * group + j
            slot = lax.rem(col - source + n_col, n_col)

            @pl.when(slot != 0)
            def _():
                to_col(pieces.at[0], pieces.at[slot], send, recv, slot).wait_recv()

            x = unpack(pieces[slot])
            a, b = halves(x)
            vec[i, :, j * piece:(j + 1) * piece] = jnp.concatenate([a, b], axis=0)

    def accumulate(v, h, l):
        both = dot(v, h)
        acc[...] += both[:16] + both[16:] + dot(v[:16], l)

    def product(i):
        accumulate(vec[i], high[i], low[i])

    for i in range(n_group):
        split(i)
    for i in range(n_group):
        gather(i, t_col, s_tcol, r_tcol)
        product(i)

    def columns(k):
        r = lax.rem(row - k + n_row, n_row)
        return pl.ds(pl.multiple_of(r * piece, LANES), piece)

    def scatter(parts, send, recv):
        copies = {}
        for k in range(1, n_row):
            r = lax.rem(row + k, n_row)
            parts[n_row + k] = pack(acc[:, pl.ds(pl.multiple_of(r * piece, LANES), piece)])
            copies[k] = go(to_row(parts.at[n_row + k], parts.at[k], send, recv, k))
        return copies

    rs = scatter(w_part, s_rs, r_rs)
    total = pack(acc[:, columns(0)])
    for k in range(1, n_row):
        rs[k].wait_recv()
        total = total + w_part[k]
    w_col[0] = total
    col_w = {k: go(to_col(w_col.at[0], w_col.at[k], s_wcol, r_wcol, k)) for k in range(1, n_col)}
    row_w = {k: go(to_row(w_col.at[0], w_row.at[k], s_wrow, r_wrow, k)) for k in range(1, n_row)}
    acc[...] = jnp.zeros_like(acc)
    mine_w = unpack(total)

    def inner(xs, ys):
        value = xs[0] * ys[0]
        for x, y in zip(xs[1:], ys[1:]):
            value = value + x * y
        return jnp.sum(value, axis=1, keepdims=True)

    lane = lax.broadcasted_iota(jnp.int32, (16, LANES), 1)
    sub = lax.broadcasted_iota(jnp.int32, (16, LANES), 0)

    def to_lanes(values):
        out = jnp.zeros((16, LANES), F32)
        for m, value in enumerate(values):
            out = jnp.where(lane == sub + 16 * m, value, out)
        return jnp.sum(out, axis=0, keepdims=True)

    def from_lanes(line, m):
        full = jnp.broadcast_to(line, (16, LANES))
        return jnp.sum(jnp.where(lane == sub + 16 * m, full, 0.0), axis=1, keepdims=True)

    tt, tw, ww = inner([mine_t], [mine_t]), inner([mine_t], [mine_w]), inner([mine_w], [mine_w])
    guess = jnp.where(ww > 0.0, tw / jnp.where(ww > 0.0, ww, 1.0), 0.0)
    near = mine_t - guess * mine_w
    moments[0] = to_lanes([tt, tw, ww, guess, inner([near], [near]), inner([near], [mine_w])])

    def to_all(lines, send, recv, k):
        other = lax.rem(row * n_col + col + k, n_dev)
        return pltpu.make_async_remote_copy(
            src_ref=lines.at[0], dst_ref=lines.at[k], send_sem=send.at[k], recv_sem=recv.at[k],
            device_id=(other // n_col, lax.rem(other, n_col)), device_id_type=MESH)

    def loop_all(act, lines, send, recv):
        def step(k, carry):
            act(to_all(lines, send, recv, k))
            return carry

        lax.fori_loop(1, n_dev, step, 0)

    loop_all(lambda c: c.start(), moments, s_mom, r_mom)

    for i in range(n_group):
        gather(i, w_col, s_wcol, r_wcol)
        product(i)

    rs2 = scatter(m_part, s_rs2, r_rs2)

    ts, ws = [mine_t], [mine_w]
    for k in range(1, n_row):
        row_t[k].wait_recv()
        row_w[k].wait_recv()
        ts.append(unpack(t_row[k]))
        ws.append(unpack(w_row[k]))
    loop_all(lambda c: c.wait_recv(), moments, s_mom, r_mom)
    known = moments[...]

    def moment(m):
        return pltpu.roll(known, LANES - 16 * m, 2) if m else known

    def total_of(value):
        return jnp.sum(value, axis=0)

    norm0_l = total_of(moment(0))
    t_k_t_l = total_of(moment(1))
    step0_l = norm0_l / t_k_t_l
    shift = step0_l[None] - moment(3)
    back = shift * moment(2)
    norm1_l = total_of(moment(4) - shift * (2.0 * moment(5) - back))
    r_w_l = total_of(moment(5) - back)
    beta_l = norm1_l / norm0_l
    fixed_l = (1.0 + beta_l) * (r_w_l + beta_l * t_k_t_l)
    step0, norm1, beta, fixed = (from_lanes(x, 0) for x in (step0_l, norm1_l, beta_l, fixed_l))

    def direction(t, w):
        r = t - step0 * w
        return r, r + beta * t

    ds = [direction(t, w)[1] for t, w in zip(ts, ws)]
    ps = [acc[:, columns(k)] for k in range(n_row)]
    finals[0] = to_lanes([inner(ds, ps)])

    loop_all(lambda c: c.start(), finals, s_fin, r_fin)

    total2 = pack(acc[:, columns(0)])
    for k in range(1, n_row):
        rs2[k].wait_recv()
        total2 = total2 + m_part[k]
    w2 = unpack(total2)
    r1, d1 = direction(mine_t, mine_w)
    mapped = (1.0 + beta) * mine_w - step0 * w2

    loop_all(lambda c: c.wait_recv(), finals, s_fin, r_fin)
    d_w2 = from_lanes(jnp.sum(finals[...], axis=0), 0)
    step1 = norm1 / (fixed - step0 * d_w2)
    both_out[0] = step0 * mine_t + step1 * d1
    both_out[1] = r1 - step1 * mapped

    for copy in started:
        copy.wait_send()

    loop_all(lambda c: c.wait_send(), moments, s_mom, r_mom)
    loop_all(lambda c: c.wait_send(), finals, s_fin, r_fin)


def apart(both, sol_out, res_out):
    classes = sol_out.shape[0]
    sol_out[...] = both[0, 0:classes, :]
    res_out[...] = both[1, 0:classes, :]


def fused(n_row, n_col, gram_matrix, targets):
    classes, piece = targets.shape
    height, width = gram_matrix.shape
    group = 1 if piece % DEPTH == 0 else 2
    n_group = n_col // group
    depth = group * piece
    packed = (SUB, piece + LANES)
    dma = pltpu.SemaphoreType.DMA
    n_dev = n_row * n_col
    vmem = pl.BlockSpec(memory_space=pltpu.VMEM)
    both = pl.pallas_call(
        functools.partial(kernel, n_row, n_col, classes, piece, group),
        out_shape=jax.ShapeDtypeStruct((2, 16, piece), F32),
        in_specs=[pl.BlockSpec(memory_space=pl.ANY), vmem],
        out_specs=vmem,
        scratch_shapes=[
            pltpu.VMEM((n_group, depth, width), F32),
            pltpu.VMEM((n_group, depth, width), BF16),
            pltpu.VMEM((n_group, depth, width), BF16),
            pltpu.VMEM((16, width), F32),
            pltpu.VMEM((n_group, 32, depth), BF16),
            pltpu.VMEM((16, piece), F32),
            pltpu.VMEM((n_col,) + packed, F32),
            pltpu.VMEM((n_row,) + packed, F32),
            pltpu.VMEM((2 * n_row,) + packed, F32),
            pltpu.VMEM((n_col,) + packed, F32),
            pltpu.VMEM((n_row,) + packed, F32),
            pltpu.VMEM((2 * n_row,) + packed, F32),
            pltpu.VMEM((n_dev, 1, LANES), F32),
            pltpu.VMEM((n_dev, 1, LANES), F32),
            dma((n_group,)),
            dma((n_col,)), dma((n_col,)), dma((n_row,)), dma((n_row,)),
            dma((n_row,)), dma((n_row,)),
            dma((n_col,)), dma((n_col,)), dma((n_row,)), dma((n_row,)),
            dma((n_row,)), dma((n_row,)),
            dma((n_dev,)), dma((n_dev,)), dma((n_dev,)), dma((n_dev,)),
        ],
        compiler_params=pltpu.CompilerParams(
            collective_id=0, has_side_effects=True, vmem_limit_bytes=60 * 2**20
        ),
    )(gram_matrix, targets)
    return pl.pallas_call(
        apart,
        out_shape=[jax.ShapeDtypeStruct(targets.shape, F32)] * 2,
        in_specs=[vmem],
        out_specs=[vmem, vmem],
    )(both)


def fits(n_row, n_col, gram_matrix, targets):
    classes, piece = targets.shape
    rest = classes - SUB
    group = 1 if piece % DEPTH == 0 else 2
    return (
        piece % LANES == 0
        and 0 < rest <= SUB
        and rest * (piece // LANES) <= SUB
        and n_col % group == 0
        and (group * piece) % DEPTH == 0
        and gram_matrix.size * 8 <= 48 * 2**20
    )


def apply_gram(gram_matrix, vectors):
    partial_value = jnp.dot(
        vectors, gram_matrix, precision=lax.Precision.HIGHEST, preferred_element_type=jnp.float32
    )
    mapped = lax.psum_scatter(partial_value, "row", scatter_dimension=1, tiled=True)
    mapped = lax.all_gather(mapped, "col", axis=1, tiled=True)
    return mapped


def class_sums(values):
    return lax.psum(values, "row")


def shards(gram_matrix, targets):
    piece_len = targets.shape[1]
    known = lax.all_gather(targets, "col", axis=1, tiled=True)
    solution = jnp.zeros_like(known)
    residual = known
    direction = known
    norm_now = class_sums(jnp.sum(residual * residual, axis=1))
    for iteration in range(ITERS):
        mapped = apply_gram(gram_matrix, direction)
        step_size = norm_now / class_sums(jnp.sum(direction * mapped, axis=1))
        solution = solution + step_size[:, None] * direction
        residual = residual - step_size[:, None] * mapped
        norm_next = class_sums(jnp.sum(residual * residual, axis=1))
        direction = residual + (norm_next / norm_now)[:, None] * direction
        norm_now = norm_next
    offset = lax.axis_index("col") * piece_len
    solution = lax.dynamic_slice_in_dim(solution, offset, piece_len, 1)
    residual = lax.dynamic_slice_in_dim(residual, offset, piece_len, 1)
    return (solution, residual)


def solution(mesh):
    n_row, n_col = mesh.shape["row"], mesh.shape["col"]

    def local(gram_matrix, targets):
        if fits(n_row, n_col, gram_matrix, targets):
            return tuple(fused(n_row, n_col, gram_matrix, targets))
        return shards(gram_matrix, targets)

    in_specs = (P("row", "col"), P(None, ("row", "col")))
    out_specs = (P(None, ("row", "col")), P(None, ("row", "col")))
    return jax.shard_map(local, mesh=mesh, in_specs=in_specs, out_specs=out_specs, check_vma=False)
```

```python
import functools

import jax
import jax.numpy as jnp
from jax import lax
from jax.experimental import pallas as pl
from jax.experimental.pallas import tpu as pltpu
from jax.sharding import PartitionSpec as P

ITERS = 2
LANES = 128
SUB = 8
DEPTH = 256
MESH = pl.DeviceIdType.MESH
F32 = jnp.float32
BF16 = jnp.bfloat16


def dot(a, b):
    return lax.dot_general(a, b, (((1,), (0,)), ((), ())), preferred_element_type=F32)


def halves(x):
    high = x.astype(BF16)
    return high, (x - high.astype(F32)).astype(BF16)


def kernel(
    n_row, n_col, classes, piece, group,
    gram, targets, both_out,
    stage, high, low, acc, vec, wide,
    t_col, t_row, w_part, w_col, w_row, m_part, moments, finals,
    gram_sem, s_tcol, r_tcol, s_trow, r_trow, s_rs, r_rs, s_wcol, r_wcol, s_wrow, r_wrow,
    s_rs2, r_rs2, s_mom, r_mom, s_fin, r_fin,
):
    row, col = lax.axis_index("row"), lax.axis_index("col")
    rest = classes - SUB
    tiles = piece // LANES
    n_dev = n_row * n_col
    n_group = n_col // group
    own_group = col // group
    depth = group * piece
    order = [0]
    for k in range(1, n_group):
        order.append((k + 1) // 2 if k % 2 else n_group - k // 2)
    groups = [lax.rem(own_group + k, n_group) for k in order]

    for i in range(n_group):
        pltpu.make_async_copy(
            gram.at[pl.ds(pl.multiple_of(groups[i] * depth, DEPTH), depth)], stage.at[i], gram_sem.at[i]
        ).start()

    barrier = pltpu.get_barrier_semaphore()

    for k in range(1, n_col):
        pl.semaphore_signal(barrier, inc=1, device_id=(row, lax.rem(col + k, n_col)), device_id_type=MESH)
    for k in range(1, n_row):
        pl.semaphore_signal(barrier, inc=1, device_id=(lax.rem(row + k, n_row), col), device_id_type=MESH)

    rows8 = lax.broadcasted_iota(jnp.int32, (SUB, LANES), 0)

    def pack(x):
        extra = jnp.zeros((SUB, LANES), F32)
        for i in range(tiles):
            part = x[SUB:, i * LANES:(i + 1) * LANES]
            if i:
                part = pltpu.roll(part, rest * i, 0)
            extra = jnp.where((rows8 >= rest * i) & (rows8 < rest * (i + 1)), part, extra)
        return jnp.concatenate([x[:SUB], extra], axis=1)

    def unpack(y):
        extra = y[:, piece:]
        parts = []
        for i in range(tiles):
            part = pltpu.roll(extra, SUB - rest * i, 0) if i else extra
            parts.append(jnp.where(rows8 < rest, part, 0.0))
        return jnp.concatenate([y[:, :piece], jnp.concatenate(parts, axis=1)], axis=0)

    def to_col(src, dst, send, recv, k):
        return pltpu.make_async_remote_copy(
            src_ref=src, dst_ref=dst, send_sem=send.at[k], recv_sem=recv.at[k],
            device_id=(row, lax.rem(col + k, n_col)), device_id_type=MESH)

    def to_row(src, dst, send, recv, k):
        return pltpu.make_async_remote_copy(
            src_ref=src, dst_ref=dst, send_sem=send.at[k], recv_sem=recv.at[k],
            device_id=(lax.rem(row + k, n_row), col), device_id_type=MESH)

    started = []
    far_first = sorted(range(1, n_col), key=lambda k: -min(k, n_col - k))

    def go(copy):
        copy.start()
        started.append(copy)
        return copy

    wide[...] = jnp.zeros_like(wide)
    wide[0:classes, :] = targets[...]
    mine_t = wide[...]
    t_col[0] = pack(mine_t)
    acc[...] = jnp.zeros_like(acc)
    pl.semaphore_wait(barrier, n_row + n_col - 2)

    col_t = {k: go(to_col(t_col.at[0], t_col.at[k], s_tcol, r_tcol, k)) for k in far_first}
    row_t = {k: go(to_row(t_col.at[0], t_row.at[k], s_trow, r_trow, k)) for k in range(1, n_row)}

    def split(i):
        pltpu.make_async_copy(gram.at[pl.ds(0, depth)], stage.at[i], gram_sem.at[i]).wait()

        def part(j, carry):
            off = pl.ds(pl.multiple_of(j * DEPTH, DEPTH), DEPTH)
            high[i, off, :], low[i, off, :] = halves(stage[i, off, :])
            return carry

        lax.fori_loop(0, depth // DEPTH, part, 0)

    def gather(i, pieces, send, recv):
        for j in range(group):
            source = groups[i] * group + j
            slot = lax.rem(col - source + n_col, n_col)

            @pl.when(slot != 0)
            def _():
                to_col(pieces.at[0], pieces.at[slot], send, recv, slot).wait_recv()

            x = unpack(pieces[slot])
            a, b = halves(x)
            vec[i, :, j * piece:(j + 1) * piece] = jnp.concatenate([a, b], axis=0)

    def accumulate(v, h, l):
        both = dot(v, h)
        acc[...] += both[:16] + both[16:] + dot(v[:16], l)

    def product(i):
        accumulate(vec[i], high[i], low[i])

    for i in range(n_group):
        split(i)
    for i in range(n_group - 1):
        gather(i, t_col, s_tcol, r_tcol)
        product(i)
    gather(n_group - 1, t_col, s_tcol, r_tcol)

    def product_of(k):
        last = n_group - 1
        r = lax.rem(row + k, n_row)
        at = pl.ds(pl.multiple_of(r * piece, LANES), piece)
        both = dot(vec[last], high[last, :, at])
        return acc[:, at] + both[:16] + both[16:] + dot(vec[last, :16], low[last, :, at])

    def columns(k):
        r = lax.rem(row - k + n_row, n_row)
        return pl.ds(pl.multiple_of(r * piece, LANES), piece)

    def scatter(parts, send, recv):
        copies = {}
        for k in range(1, n_row):
            r = lax.rem(row + k, n_row)
            parts[n_row + k] = pack(acc[:, pl.ds(pl.multiple_of(r * piece, LANES), piece)])
            copies[k] = go(to_row(parts.at[n_row + k], parts.at[k], send, recv, k))
        return copies

    rs = {}
    for k in range(1, n_row):
        w_part[n_row + k] = pack(product_of(k))
        rs[k] = go(to_row(w_part.at[n_row + k], w_part.at[k], s_rs, r_rs, k))
    total = pack(product_of(0))
    for k in range(1, n_row):
        rs[k].wait_recv()
        total = total + w_part[k]
    w_col[0] = total
    row_w = {k: go(to_row(w_col.at[0], w_row.at[k], s_wrow, r_wrow, k)) for k in range(1, n_row)}
    col_w = {k: go(to_col(w_col.at[0], w_col.at[k], s_wcol, r_wcol, k)) for k in far_first}
    acc[...] = jnp.zeros_like(acc)
    mine_w = unpack(total)

    def inner(xs, ys):
        value = xs[0] * ys[0]
        for x, y in zip(xs[1:], ys[1:]):
            value = value + x * y
        return jnp.sum(value, axis=1, keepdims=True)

    lane = lax.broadcasted_iota(jnp.int32, (16, LANES), 1)
    sub = lax.broadcasted_iota(jnp.int32, (16, LANES), 0)

    def to_lanes(values):
        out = jnp.zeros((16, LANES), F32)
        for m, value in enumerate(values):
            out = jnp.where(lane == sub + 16 * m, value, out)
        return jnp.sum(out, axis=0, keepdims=True)

    def from_lanes(line, m):
        full = jnp.broadcast_to(line, (16, LANES))
        return jnp.sum(jnp.where(lane == sub + 16 * m, full, 0.0), axis=1, keepdims=True)

    tt, tw, ww = inner([mine_t], [mine_t]), inner([mine_t], [mine_w]), inner([mine_w], [mine_w])
    guess = jnp.where(ww > 0.0, tw / jnp.where(ww > 0.0, ww, 1.0), 0.0)
    near = mine_t - guess * mine_w
    moments[0] = to_lanes([tt, tw, ww, guess, inner([near], [near]), inner([near], [mine_w])])

    def to_all(lines, send, recv, k):
        other = lax.rem(row * n_col + col + k, n_dev)
        return pltpu.make_async_remote_copy(
            src_ref=lines.at[0], dst_ref=lines.at[k], send_sem=send.at[k], recv_sem=recv.at[k],
            device_id=(other // n_col, lax.rem(other, n_col)), device_id_type=MESH)

    def loop_all(act, lines, send, recv):
        def step(k, carry):
            act(to_all(lines, send, recv, k))
            return carry

        for k in range(1, n_dev):
            step(k, 0)

    loop_all(lambda c: c.start(), moments, s_mom, r_mom)

    for i in range(n_group - 1):
        gather(i, w_col, s_wcol, r_wcol)
        product(i)

    ts, ws = [mine_t], [mine_w]
    for k in range(1, n_row):
        row_t[k].wait_recv()
        row_w[k].wait_recv()
        ts.append(unpack(t_row[k]))
        ws.append(unpack(w_row[k]))
    loop_all(lambda c: c.wait_recv(), moments, s_mom, r_mom)
    known = moments[...]

    def moment(m):
        return pltpu.roll(known, LANES - 16 * m, 2) if m else known

    def total_of(value):
        return jnp.sum(value, axis=0)

    norm0_l = total_of(moment(0))
    t_k_t_l = total_of(moment(1))
    step0_l = norm0_l / t_k_t_l
    shift = step0_l[None] - moment(3)
    back = shift * moment(2)
    norm1_l = total_of(moment(4) - shift * (2.0 * moment(5) - back))
    r_w_l = total_of(moment(5) - back)
    beta_l = norm1_l / norm0_l
    fixed_l = (1.0 + beta_l) * (r_w_l + beta_l * t_k_t_l)
    step0, norm1, beta, fixed = (from_lanes(x, 0) for x in (step0_l, norm1_l, beta_l, fixed_l))

    def direction(t, w):
        r = t - step0 * w
        return r, r + beta * t

    ds = [direction(t, w)[1] for t, w in zip(ts, ws)]
    gather(n_group - 1, w_col, s_wcol, r_wcol)
    product(n_group - 1)
    ps = [acc[:, columns(k)] for k in range(n_row)]
    finals[0] = to_lanes([inner(ds, ps)])

    loop_all(lambda c: c.start(), finals, s_fin, r_fin)

    rs2 = scatter(m_part, s_rs2, r_rs2)
    total2 = pack(acc[:, columns(0)])
    for k in range(1, n_row):
        rs2[k].wait_recv()
        total2 = total2 + m_part[k]
    w2 = unpack(total2)
    r1, d1 = direction(mine_t, mine_w)
    mapped = (1.0 + beta) * mine_w - step0 * w2

    loop_all(lambda c: c.wait_recv(), finals, s_fin, r_fin)
    d_w2 = from_lanes(jnp.sum(finals[...], axis=0), 0)
    step1 = norm1 / (fixed - step0 * d_w2)
    both_out[0] = step0 * mine_t + step1 * d1
    both_out[1] = r1 - step1 * mapped

    for copy in started:
        copy.wait_send()

    loop_all(lambda c: c.wait_send(), moments, s_mom, r_mom)
    loop_all(lambda c: c.wait_send(), finals, s_fin, r_fin)


def apart(both, sol_out, res_out):
    classes = sol_out.shape[0]
    sol_out[...] = both[0, 0:classes, :]
    res_out[...] = both[1, 0:classes, :]


def fused(n_row, n_col, gram_matrix, targets):
    classes, piece = targets.shape
    height, width = gram_matrix.shape
    group = 1 if piece % DEPTH == 0 else 2
    n_group = n_col // group
    depth = group * piece
    packed = (SUB, piece + LANES)
    dma = pltpu.SemaphoreType.DMA
    n_dev = n_row * n_col
    vmem = pl.BlockSpec(memory_space=pltpu.VMEM)
    both = pl.pallas_call(
        functools.partial(kernel, n_row, n_col, classes, piece, group),
        out_shape=jax.ShapeDtypeStruct((2, 16, piece), F32),
        in_specs=[pl.BlockSpec(memory_space=pl.ANY), vmem],
        out_specs=vmem,
        scratch_shapes=[
            pltpu.VMEM((n_group, depth, width), F32),
            pltpu.VMEM((n_group, depth, width), BF16),
            pltpu.VMEM((n_group, depth, width), BF16),
            pltpu.VMEM((16, width), F32),
            pltpu.VMEM((n_group, 32, depth), BF16),
            pltpu.VMEM((16, piece), F32),
            pltpu.VMEM((n_col,) + packed, F32),
            pltpu.VMEM((n_row,) + packed, F32),
            pltpu.VMEM((2 * n_row,) + packed, F32),
            pltpu.VMEM((n_col,) + packed, F32),
            pltpu.VMEM((n_row,) + packed, F32),
            pltpu.VMEM((2 * n_row,) + packed, F32),
            pltpu.VMEM((n_dev, 1, LANES), F32),
            pltpu.VMEM((n_dev, 1, LANES), F32),
            dma((n_group,)),
            dma((n_col,)), dma((n_col,)), dma((n_row,)), dma((n_row,)),
            dma((n_row,)), dma((n_row,)),
            dma((n_col,)), dma((n_col,)), dma((n_row,)), dma((n_row,)),
            dma((n_row,)), dma((n_row,)),
            dma((n_dev,)), dma((n_dev,)), dma((n_dev,)), dma((n_dev,)),
        ],
        compiler_params=pltpu.CompilerParams(
            collective_id=0, has_side_effects=True, vmem_limit_bytes=60 * 2**20
        ),
    )(gram_matrix, targets)
    return pl.pallas_call(
        apart,
        out_shape=[jax.ShapeDtypeStruct(targets.shape, F32)] * 2,
        in_specs=[vmem],
        out_specs=[vmem, vmem],
    )(both)


def fits(n_row, n_col, gram_matrix, targets):
    classes, piece = targets.shape
    rest = classes - SUB
    group = 1 if piece % DEPTH == 0 else 2
    return (
        piece % LANES == 0
        and 0 < rest <= SUB
        and rest * (piece // LANES) <= SUB
        and n_col % group == 0
        and (group * piece) % DEPTH == 0
        and gram_matrix.size * 8 <= 48 * 2**20
    )


def apply_gram(gram_matrix, vectors):
    partial_value = jnp.dot(
        vectors, gram_matrix, precision=lax.Precision.HIGHEST, preferred_element_type=jnp.float32
    )
    mapped = lax.psum_scatter(partial_value, "row", scatter_dimension=1, tiled=True)
    mapped = lax.all_gather(mapped, "col", axis=1, tiled=True)
    return mapped


def class_sums(values):
    return lax.psum(values, "row")


def shards(gram_matrix, targets):
    piece_len = targets.shape[1]
    known = lax.all_gather(targets, "col", axis=1, tiled=True)
    solution = jnp.zeros_like(known)
    residual = known
    direction = known
    norm_now = class_sums(jnp.sum(residual * residual, axis=1))
    for iteration in range(ITERS):
        mapped = apply_gram(gram_matrix, direction)
        step_size = norm_now / class_sums(jnp.sum(direction * mapped, axis=1))
        solution = solution + step_size[:, None] * direction
        residual = residual - step_size[:, None] * mapped
        norm_next = class_sums(jnp.sum(residual * residual, axis=1))
        direction = residual + (norm_next / norm_now)[:, None] * direction
        norm_now = norm_next
    offset = lax.axis_index("col") * piece_len
    solution = lax.dynamic_slice_in_dim(solution, offset, piece_len, 1)
    residual = lax.dynamic_slice_in_dim(residual, offset, piece_len, 1)
    return (solution, residual)


def solution(mesh):
    n_row, n_col = mesh.shape["row"], mesh.shape["col"]

    def local(gram_matrix, targets):
        if fits(n_row, n_col, gram_matrix, targets):
            return tuple(fused(n_row, n_col, gram_matrix, targets))
        return shards(gram_matrix, targets)

    in_specs = (P("row", "col"), P(None, ("row", "col")))
    out_specs = (P(None, ("row", "col")), P(None, ("row", "col")))
    return jax.shard_map(local, mesh=mesh, in_specs=in_specs, out_specs=out_specs, check_vma=False)
```
